256 devices in a mesh: grp: 8 (over x, core), lat: 32 (over z, y).
Axes of the slice: x: 4, y: 4, z: 8, core: 2. Of those that a mesh axis runs over, the one named last changes fastest.
Arguments:
- coefficients: bfloat16 [192, 12288, 256], P('grp', 'lat'), may hold values from -6 to 6
- leaf: bfloat16 [192, 4096, 384], P('grp', 'lat'), may hold values from -0.3125 to 0.3125
- mix_self: bfloat16 [192, 5, 4096, 128], P('grp', None, 'lat'), may hold values from -0.375 to 0.375
- mix_partner: bfloat16 [192, 5, 2048, 128], P('grp', None, 'lat'), may hold values from -0.5 to 0.5
- skeleton: int32 [192, 5, 2048], P('grp', None, 'lat'), may hold values from 0 to 127, as said below
- expand: bfloat16 [192, 2048, 128], P('grp', 'lat'), may hold values from -0.5 to 0.5
- slot_order: int32 [192], replicated, may hold values from -1 to 143, as said below
Outputs:
- field: bfloat16 [256, 2048, 128], P('grp', 'lat')
The draws below stay inside these ranges and needn't reach their ends.
Inputs may be any that keep to these rules, and one draw needn't show every extreme that they name: `slot_order`: each order 0 to 143 stands in exactly one slot, all other slots hold -1; in every draw some group of 24 slots is full. `skeleton`: for each slot, level and block the 64 indices are distinct.
All inputs are finite; a program needn't handle non-finite values.
Results may differ from the reference program's by a relative error of at most 0.012.
Values may be sent and summed in bfloat16 or wider, within the bound.
A program may use at most 64 MiB of HBM per device.

```python
import math
import jax
import jax.numpy as jnp
from jax import lax

SHELLS = 128
RANK = 64
DEG_DEV = 384
CAP = 24
LAT_DEV = 64
LEVELS = 5
SLOTS = 192
ORDERS = 144
DEGREES = 12288
NLAT = 2048
NLON = 256
N_LAT = 32


def draw_slot_order(key, part):
    first, second, third = jax.random.split(jax.random.fold_in(key, 11), 3)
    full_group = jax.random.randint(first, (), 0, SLOTS // CAP)
    group = jnp.arange(SLOTS, dtype=jnp.int32) // CAP
    shuffle = jax.random.permutation(second, SLOTS).astype(jnp.int32)
    priority = jnp.where(group == full_group, 0, SLOTS) + shuffle
    chosen = jnp.argsort(priority, stable=True)[:ORDERS]
    orders = jax.random.permutation(third, ORDERS).astype(jnp.int32)
    result = jnp.full((SLOTS,), -1, jnp.int32)
    return result.at[chosen].set(orders)


def draw_skeleton(key, part):
    noise = jax.random.randint(jax.random.fold_in(key, 7), (SLOTS, LEVELS, N_LAT, 2 * RANK), 0, 2 ** 20)
    scores = noise * (2 * RANK) + jnp.arange(2 * RANK, dtype=jnp.int32)
    picked = jnp.argsort(scores, axis=-1, stable=True)[..., :RANK]
    return picked.reshape(SLOTS, LEVELS, N_LAT * RANK).astype(jnp.int32)


def block_levels(stream_key, dims, shards, least, top_value):
    level, own = 1.0, jax.random.fold_in(stream_key, 6)
    for axis_at, shards_of in shards:
        steps = jnp.exp(jax.random.uniform(jax.random.fold_in(own, axis_at), (shards_of,), jnp.float32, least / len(shards), top_value / len(shards)))
        level = level * jnp.repeat(steps, dims[axis_at] // shards_of).reshape([-1 if axis == axis_at else 1 for axis in range(len(dims))])
    return level


def bell_draw(rng, dims, spread, limit, cuts=(), kind=jnp.bfloat16):
    factor_of = block_levels(rng, dims, cuts, -0.22, 0.18) if cuts else 1.0
    drawn = jax.random.normal(rng, dims, jnp.float32) * spread * factor_of
    return jnp.minimum(jnp.maximum(drawn, -limit), limit).astype(kind)


def setup_inputs(seed: int = 0) -> dict:
    seeds = jax.random.split(jax.random.key(seed), 8)
    return {
        "coefficients": bell_draw(seeds[0], (SLOTS, DEGREES, 2 * SHELLS), 1.0, 6.0, ((0, 8), (1, 32))),
        "leaf": bell_draw(seeds[1], (SLOTS, N_LAT * 2 * RANK, DEG_DEV), DEG_DEV ** -0.5, 0.3125, ((0, 8), (1, 32))),
        "mix_self": bell_draw(seeds[2], (SLOTS, LEVELS, N_LAT * 2 * RANK, 2 * RANK), (4 * RANK) ** -0.5, 0.375, ((0, 8), (2, 32))),
        "mix_partner": bell_draw(seeds[3], (SLOTS, LEVELS, N_LAT * RANK, 2 * RANK), (2 * RANK) ** -0.5, 0.5, ((0, 8), (2, 32))),
        "skeleton": draw_skeleton(jax.random.fold_in(seeds[7], 71), 0),
        "expand": bell_draw(seeds[5], (SLOTS, NLAT, 2 * RANK), (2 * RANK) ** -0.5, 0.5, ((0, 8), (1, 32))),
        "slot_order": draw_slot_order(jax.random.fold_in(seeds[7], 71), 0),
    }


def pick_rows(block, wanted):
    return block[wanted]

def trig_tables(orders, lon_start, lon_count, lon_total, scale):
    column = lon_start + jnp.arange(lon_count, dtype=jnp.int32)
    live = orders >= 0
    degree = jnp.maximum(orders, 0).astype(jnp.int32)
    remain = degree[:, None] * column[None, :] % lon_total
    angle = 2.0 * math.pi * remain.astype(jnp.float32) / lon_total
    cos_table = jnp.where(live[:, None], jnp.cos(angle) * scale, 0.0).astype(jnp.bfloat16)
    sin_table = jnp.where(live[:, None], -jnp.sin(angle) * scale, 0.0).astype(jnp.bfloat16)
    return (cos_table, sin_table)

def one_slot(inputs):
    coeff, leaf_q, self_q, partner_q, skel_q, expand_q = inputs
    source = coeff.astype(jnp.float32).reshape(N_LAT, DEG_DEV, 2 * SHELLS)
    factor = leaf_q.astype(jnp.float32).reshape(N_LAT, 2 * RANK, DEG_DEV)
    state = jnp.einsum('bad,bds->bas', factor, source).astype(jnp.bfloat16)
    self_all = self_q.astype(jnp.float32).reshape(LEVELS, N_LAT, 2 * RANK, 2 * RANK)
    partner_all = partner_q.astype(jnp.float32).reshape(LEVELS, N_LAT, RANK, 2 * RANK)
    skel_all = skel_q.reshape(LEVELS, N_LAT, RANK).astype(jnp.int32)
    blocks = jnp.arange(N_LAT, dtype=jnp.int32)
    for level in range(LEVELS):
        other = state[jnp.bitwise_xor(blocks, 1 << level)]
        picked = jax.vmap(pick_rows)(other, skel_all[level])
        mixed = jnp.einsum('bac,bcs->bas', self_all[level], state.astype(jnp.float32))
        mixed = mixed + jnp.einsum('bra,brs->bas', partner_all[level], picked.astype(jnp.float32))
        state = mixed.astype(jnp.bfloat16)
    final = expand_q.astype(jnp.float32).reshape(N_LAT, LAT_DEV, 2 * RANK)
    fields = jnp.einsum('bla,bas->bls', final, state.astype(jnp.float32)).astype(jnp.bfloat16)
    return fields.reshape(NLAT, 2 * SHELLS)

def reference(coefficients, leaf, mix_self, mix_partner, skeleton, expand, slot_order):
    fields_all = lax.map(one_slot, (coefficients, leaf, mix_self, mix_partner, skeleton, expand))
    scale = 1.0 / math.sqrt(ORDERS)
    cos_table, sin_table = trig_tables(slot_order, 0, NLON, NLON, scale)
    cos_wide = cos_table.astype(jnp.float32)
    sin_wide = sin_table.astype(jnp.float32)
    bands = jnp.transpose(fields_all.reshape(SLOTS, N_LAT, LAT_DEV, 2 * SHELLS), (1, 0, 2, 3))

    def one_band(band):
        wide = band.astype(jnp.float32)
        total = jnp.einsum('kls,kj->jls', wide[:, :, :SHELLS], cos_wide)
        total = total + jnp.einsum('kls,kj->jls', wide[:, :, SHELLS:], sin_wide)
        return total.astype(jnp.bfloat16)
    result = lax.map(one_band, bands)
    return jnp.transpose(result, (1, 0, 2, 3)).reshape(NLON, NLAT, SHELLS)
```

```python
import functools
import math

import jax
import jax.numpy as jnp
from jax import lax
from jax.experimental import pallas as pl
from jax.experimental.pallas import tpu as pltpu
from jax.sharding import PartitionSpec as P

LON_DEV = 32
GROUP = 3
MESH = pl.DeviceIdType.MESH
F32 = jnp.float32
BF16 = jnp.bfloat16


def dot(a, b):
    return jnp.dot(a, b, preferred_element_type=F32)


def dot_rows(a, b):
    return lax.dot_general(a, b, (((0,), (0,)), ((), ())), preferred_element_type=F32)


def kernel(
    levels, groups, gsize,
    coeff_h, leaf_h, self_h, partner_h, skel_ref, expand_h, order_ref, out_h,
    coeff_v, leaf_v, self_v, partner_v, expand_v,
    ask_send, ask_recv, state, send_v, recv_v,
    fields, pieces, pieces_w, whole_w, whole,
    in_sem, ask_ssem, ask_rsem, ssem, rsem, fssem, frsem, ossem, orsem, own_sem,
):
    slots, width = state.shape[0], state.shape[1]
    half = coeff_v.shape[2] // 2
    chunks = slots // gsize
    lat_part = fields.shape[2]
    grp = lax.axis_index("grp")
    lat = lax.axis_index("lat")
    partners = []
    for k in range(levels):
        mask = 2**k
        partners.append(lat + (1 - 2 * ((lat // mask) % 2)) * mask)
    others = [(grp + d) % groups for d in range(1, groups)]
    senders = [(grp + groups - d) % groups for d in range(1, groups)]

    def span(c):
        return pl.ds(c * gsize, gsize)

    loads = (
        (coeff_h, coeff_v), (leaf_h, leaf_v), (self_h, self_v),
        (partner_h, partner_v), (expand_h, expand_v),
    )

    def load(i, c):
        source, target = loads[i]
        return pltpu.make_async_copy(source.at[span(c)], target.at[span(c)], in_sem.at[i, c])

    def start_loads(c, _):
        for i in range(len(loads)):
            load(i, c).start()
        return 0

    lax.fori_loop(0, chunks, start_loads, 0)

    barrier = pltpu.get_barrier_semaphore()
    for k in range(levels):
        pl.semaphore_signal(barrier, inc=1, device_id={"lat": partners[k]}, device_id_type=MESH)
    for other in others:
        pl.semaphore_signal(barrier, inc=1, device_id={"grp": other}, device_id_type=MESH)
    for k in range(levels):
        ask_send[k] = skel_ref[:, k, :]
    pl.semaphore_wait(barrier, levels + groups - 1)

    def ask(k):
        return pltpu.make_async_remote_copy(
            src_ref=ask_send.at[k], dst_ref=ask_recv.at[k],
            send_sem=ask_ssem.at[k], recv_sem=ask_rsem.at[k],
            device_id={"lat": partners[k]}, device_id_type=MESH,
        )

    for k in range(levels):
        ask(k).start()

    def exchange(k, c):
        return pltpu.make_async_remote_copy(
            src_ref=send_v.at[k, span(c)], dst_ref=recv_v.at[k, span(c)],
            send_sem=ssem.at[k], recv_sem=rsem.at[k, c],
            device_id={"lat": partners[k]}, device_id_type=MESH,
        )

    def hand_over(d, c):
        return pltpu.make_async_remote_copy(
            src_ref=fields.at[others[d], span(c)], dst_ref=pieces.at[grp, span(c)],
            send_sem=fssem.at[d], recv_sem=frsem.at[d],
            device_id={"grp": others[d]}, device_id_type=MESH,
        )

    row_of = lax.broadcasted_iota(jnp.int32, (width, ask_recv.shape[2]), 0)

    def stage(k, c):
        if k == 0:
            load(0, c).wait()
            load(1, c).wait()
        else:
            if k == 1:
                load(2, c).wait()
                load(3, c).wait()
            if k == levels:
                load(4, c).wait()
            exchange(k - 1, c).wait_recv()
        for i in range(gsize):
            q = c * gsize + i
            if k == 0:
                now = dot(leaf_v[q], coeff_v[q]).astype(BF16)
            else:
                mixed = dot(self_v[q, k - 1], state[q])
                mixed = mixed + dot_rows(partner_v[q, k - 1], recv_v[k - 1, q])
                now = mixed.astype(BF16)
            if k < levels:
                wanted = ask_recv[k, pl.ds(q, 1), :]
                pick = (row_of == wanted).astype(F32).astype(BF16)
                send_v[k, q] = dot_rows(pick, now).astype(BF16)
                state[q] = now
            else:
                field = dot(expand_v[q], now).astype(BF16)
                for g in range(groups):
                    fields[g, q] = field[g * lat_part:(g + 1) * lat_part]
        if k < levels:
            exchange(k, c).start()
        else:
            for d in range(groups - 1):
                hand_over(d, c).start()

    def step(t, _):
        for k in range(levels + 1):
            c = t - k

            @pl.when((c >= 0) & (c < chunks))
            def _():
                if k < levels:
                    @pl.when(c == 0)
                    def _():
                        ask(k).wait_recv()

                stage(k, c)
        return 0

    lax.fori_loop(0, chunks + levels, step, 0)

    lons = whole.shape[0]
    total = groups * slots
    order = order_ref[...]
    turn = lax.broadcasted_iota(jnp.int32, (lons, total), 0)
    turn = (jnp.maximum(order, 0) * turn) % lons
    angle = 2.0 * math.pi * turn.astype(F32) / lons
    scale = jnp.where(order >= 0, 1.0 / math.sqrt(total * 3 // 4), 0.0)
    cos_table = (jnp.cos(angle) * scale).astype(BF16)
    sin_table = (-jnp.sin(angle) * scale).astype(BF16)

    pieces_w[pl.ds(grp * slots, slots)] = fields[grp].astype(F32)
    for d in range(groups - 1):
        pltpu.make_async_remote_copy(
            src_ref=fields.at[others[d]], dst_ref=pieces.at[senders[d]],
            send_sem=fssem.at[d], recv_sem=frsem.at[d],
            device_id={"grp": others[d]}, device_id_type=MESH,
        ).wait_recv()
        pieces_w[pl.ds(senders[d] * slots, slots)] = pieces[senders[d]].astype(F32)

    for row in range(0, lat_part, 2):
        cos_part, sin_part = [], []
        for at in (row, row + 1):
            cos_part.append(pieces_w[:, at, :half])
            sin_part.append(pieces_w[:, at, half:])
        mapped = dot(cos_table, jnp.concatenate(cos_part, axis=1).astype(BF16))
        mapped = mapped + dot(sin_table, jnp.concatenate(sin_part, axis=1).astype(BF16))
        whole_w[:, row, :] = mapped[:, :half]
        whole_w[:, row + 1, :] = mapped[:, half:]
    whole[...] = whole_w[...].astype(BF16)

    lon_dev = lons // groups

    def scatter(d):
        return pltpu.make_async_remote_copy(
            src_ref=whole.at[pl.ds(others[d] * lon_dev, lon_dev)],
            dst_ref=out_h.at[:, pl.ds(grp * lat_part, lat_part), :],
            send_sem=ossem.at[d], recv_sem=orsem.at[d],
            device_id={"grp": others[d]}, device_id_type=MESH,
        )

    for d in range(groups - 1):
        scatter(d).start()
    own = pltpu.make_async_copy(
        whole.at[pl.ds(grp * lon_dev, lon_dev)],
        out_h.at[:, pl.ds(grp * lat_part, lat_part), :], own_sem,
    )
    own.start()
    own.wait()
    for k in range(levels):
        ask(k).wait_send()
        pltpu.make_async_remote_copy(
            src_ref=send_v.at[k], dst_ref=recv_v.at[k],
            send_sem=ssem.at[k], recv_sem=rsem.at[k, 0],
            device_id={"lat": partners[k]}, device_id_type=MESH,
        ).wait_send()
    for d in range(groups - 1):
        pltpu.make_async_remote_copy(
            src_ref=fields.at[others[d]], dst_ref=pieces.at[grp],
            send_sem=fssem.at[d], recv_sem=frsem.at[d],
            device_id={"grp": others[d]}, device_id_type=MESH,
        ).wait_send()
        scatter(d).wait_send()
        pltpu.make_async_remote_copy(
            src_ref=whole.at[pl.ds(others[d] * lon_dev, lon_dev)],
            dst_ref=out_h.at[:, pl.ds(senders[d] * lat_part, lat_part), :],
            send_sem=ossem.at[d], recv_sem=orsem.at[d],
            device_id={"grp": others[d]}, device_id_type=MESH,
        ).wait_recv()


def on_device(coefficients, leaf, mix_self, mix_partner, skeleton, expand, slot_order):
    slots, _, columns = coefficients.shape
    width = leaf.shape[1]
    rank = mix_partner.shape[2]
    lats = expand.shape[1]
    levels = lax.axis_size("lat").bit_length() - 1
    groups = lax.axis_size("grp")
    lons = LON_DEV * groups
    half = columns // 2
    part = lats // groups
    chunks = slots // GROUP
    dma = pltpu.SemaphoreType.DMA
    anywhere = pl.BlockSpec(memory_space=pl.ANY)
    vmem = pl.BlockSpec(memory_space=pltpu.VMEM)
    return pl.pallas_call(
        functools.partial(kernel, levels, groups, GROUP),
        out_shape=jax.ShapeDtypeStruct((LON_DEV, lats, half), BF16),
        in_specs=[anywhere, anywhere, anywhere, anywhere, vmem, anywhere, vmem],
        out_specs=anywhere,
        scratch_shapes=[
            pltpu.VMEM(coefficients.shape, BF16),
            pltpu.VMEM(leaf.shape, BF16),
            pltpu.VMEM(mix_self.shape, BF16),
            pltpu.VMEM(mix_partner.shape, BF16),
            pltpu.VMEM(expand.shape, BF16),
            pltpu.VMEM((levels, slots, rank), jnp.int32),
            pltpu.VMEM((levels, slots, rank), jnp.int32),
            pltpu.VMEM((slots, width, columns), BF16),
            pltpu.VMEM((levels, slots, rank, columns), BF16),
            pltpu.VMEM((levels, slots, rank, columns), BF16),
            pltpu.VMEM((groups, slots, part, columns), BF16),
            pltpu.VMEM((groups, slots, part, columns), BF16),
            pltpu.VMEM((groups * slots, part, columns), F32),
            pltpu.VMEM((lons, part, half), F32),
            pltpu.VMEM((lons, part, half), BF16),
            dma((5, chunks)),
            dma((levels,)), dma((levels,)),
            dma((levels,)), dma((levels, chunks)),
            dma((groups - 1,)), dma((groups - 1,)),
            dma((groups - 1,)), dma((groups - 1,)),
            dma,
        ],
        compiler_params=pltpu.CompilerParams(
            collective_id=0, has_side_effects=True, vmem_limit_bytes=48 * 1024 * 1024
        ),
        name="synthesis",
    )(coefficients, leaf, mix_self, mix_partner, skeleton, expand, slot_order[None, :])


def solution(mesh):
    return jax.shard_map(
        on_device,
        mesh=mesh,
        in_specs=(
            P("grp", "lat", None),
            P("grp", "lat", None),
            P("grp", None, "lat", None),
            P("grp", None, "lat", None),
            P("grp", None, "lat"),
            P("grp", "lat", None),
            P(),
        ),
        out_specs=P("grp", "lat", None),
        check_vma=False,
    )
```

```python
import functools
import math

import jax
import jax.numpy as jnp
from jax import lax
from jax.experimental import pallas as pl
from jax.experimental.pallas import tpu as pltpu
from jax.sharding import PartitionSpec as P

LON_DEV = 32
GROUP = 1
STRIDE = 2
AHEAD = 4
STAGES = lambda levels: range(levels + 1)
MESH = pl.DeviceIdType.MESH
F32 = jnp.float32
BF16 = jnp.bfloat16


def dot(a, b):
    return jnp.dot(a, b, preferred_element_type=F32)


def dot_rows(a, b):
    return lax.dot_general(a, b, (((0,), (0,)), ((), ())), preferred_element_type=F32)


def kernel(
    levels, groups, gsize,
    coeff_h, leaf_h, self_h, partner_h, skel_h, expand_h, order_h, out_h,
    coeff_v, leaf_v, self_v, partner_v, expand_v,
    order_v, ask_send, ask_recv, state, send_v, recv_v,
    fields, pieces, pieces_w, whole_w, whole, cos_v, sin_v,
    in_sem, small_sem, ask_ssem, ask_rsem, ssem, rsem, fssem, frsem, ossem, orsem, own_sem,
):
    slots, width = state.shape[0], state.shape[1]
    half = coeff_v.shape[2] // 2
    chunks = slots // gsize
    lat_part = fields.shape[2]
    grp = lax.axis_index("grp")
    lat = lax.axis_index("lat")
    partners = []
    for k in range(levels):
        mask = 2**k
        partners.append(lat + (1 - 2 * ((lat // mask) % 2)) * mask)
    others = [(grp + d) % groups for d in range(1, groups)]
    senders = [(grp + groups - d) % groups for d in range(1, groups)]

    def span(c):
        return pl.ds(c * gsize, gsize)

    loads = (
        (coeff_h, coeff_v), (leaf_h, leaf_v), (self_h, self_v),
        (partner_h, partner_v), (expand_h, expand_v),
    )

    def load(i, c):
        source, target = loads[i]
        return pltpu.make_async_copy(source.at[span(c)], target.at[span(c)], in_sem.at[i, c])

    def start_loads(c, _):
        for i in range(len(loads)):
            load(i, c).start()
        return 0

    get_skel = pltpu.make_async_copy(skel_h, ask_send, small_sem.at[0])
    get_order = pltpu.make_async_copy(order_h, order_v, small_sem.at[1])
    get_skel.start()
    get_order.start()
    for c in range(min(AHEAD, chunks)):
        start_loads(c, 0)

    barrier = pltpu.get_barrier_semaphore()
    for k in range(levels):
        pl.semaphore_signal(barrier, inc=1, device_id={"lat": partners[k]}, device_id_type=MESH)
    for other in others:
        pl.semaphore_signal(barrier, inc=1, device_id={"grp": other}, device_id_type=MESH)
    get_skel.wait()
    pl.semaphore_wait(barrier, levels + groups - 1)

    def ask(k):
        return pltpu.make_async_remote_copy(
            src_ref=ask_send.at[k], dst_ref=ask_recv.at[k],
            send_sem=ask_ssem.at[k], recv_sem=ask_rsem.at[k],
            device_id={"lat": partners[k]}, device_id_type=MESH,
        )

    for k in range(levels):
        ask(k).start()

    lons = whole.shape[0]
    total = groups * slots
    get_order.wait()
    order = order_v[...]
    turn = lax.broadcasted_iota(jnp.int32, (lons, total), 0)
    turn = (jnp.maximum(order, 0) * turn) & (lons - 1)
    angle = 2.0 * math.pi * turn.astype(F32) / lons
    scale = jnp.where(order >= 0, 1.0 / math.sqrt(total * 3 // 4), 0.0)
    cos_v[...] = (jnp.cos(angle) * scale).astype(BF16)
    sin_v[...] = (-jnp.sin(angle) * scale).astype(BF16)

    def exchange(k, c):
        return pltpu.make_async_remote_copy(
            src_ref=send_v.at[k, span(c)], dst_ref=recv_v.at[k, span(c)],
            send_sem=ssem.at[k], recv_sem=rsem.at[k, c],
            device_id={"lat": partners[k]}, device_id_type=MESH,
        )

    def hand_over(d, c):
        return pltpu.make_async_remote_copy(
            src_ref=fields.at[others[d], span(c)], dst_ref=pieces.at[grp, span(c)],
            send_sem=fssem.at[d], recv_sem=frsem.at[d],
            device_id={"grp": others[d]}, device_id_type=MESH,
        )

    row_of = lax.broadcasted_iota(jnp.int32, (width, ask_recv.shape[2]), 0)

    def stage(k, c):
        if k == 0:
            load(0, c).wait()
            load(1, c).wait()
        else:
            if k == 1:
                load(2, c).wait()
                load(3, c).wait()
            if k == levels:
                load(4, c).wait()
            exchange(k - 1, c).wait_recv()
        for i in range(gsize):
            q = c * gsize + i
            if k == 0:
                now = dot(leaf_v[q], coeff_v[q]).astype(BF16)
            else:
                mixed = dot(self_v[q, k - 1], state[q])
                mixed = mixed + dot_rows(partner_v[q, k - 1], recv_v[k - 1, q])
                now = mixed.astype(BF16)
            if k < levels:
                wanted = ask_recv[k, pl.ds(q, 1), :]
                pick = (row_of == wanted).astype(F32).astype(BF16)
                send_v[k, q] = dot_rows(pick, now).astype(BF16)
                state[q] = now
            else:
                field = dot(expand_v[q], now).astype(BF16)
                for g in range(groups):
                    fields[g, q] = field[g * lat_part:(g + 1) * lat_part]
        if k < levels:
            exchange(k, c).start()
        else:
            for d in range(groups - 1):
                hand_over(d, c).start()

    def step(t, _):
        @pl.when(t + AHEAD < chunks)
        def _():
            start_loads(t + AHEAD, 0)

        for k in STAGES(levels):
            c = t - k * STRIDE

            @pl.when((c >= 0) & (c < chunks))
            def _():
                if k < levels:
                    @pl.when(c == 0)
                    def _():
                        ask(k).wait_recv()

                stage(k, c)
        return 0

    lax.fori_loop(0, chunks + levels * STRIDE, step, 0)

    def widen(block, value):
        rows = slots * lat_part
        flat = value.astype(F32).reshape(rows, 2 * half)
        for part in range(2):
            pieces_w[part, pl.ds(block * rows, rows), :] = flat[:, part * half:(part + 1) * half]

    widen(grp, fields[grp])
    for d in range(groups - 1):
        pltpu.make_async_remote_copy(
            src_ref=fields.at[others[d]], dst_ref=pieces.at[senders[d]],
            send_sem=fssem.at[d], recv_sem=frsem.at[d],
            device_id={"grp": others[d]}, device_id_type=MESH,
        ).wait_recv()
        widen(senders[d], pieces[senders[d]])

    cos_table, sin_table = cos_v[...], sin_v[...]
    for row in range(0, lat_part, 2):
        parts = []
        for part in range(2):
            pair = [pieces_w[part, pl.ds(row + at, total, stride=lat_part), :] for at in range(2)]
            parts.append(jnp.concatenate(pair, axis=1).astype(BF16))
        mapped = dot(cos_table, parts[0]) + dot(sin_table, parts[1])
        for at in range(2):
            whole_w[pl.ds(row + at, lons, stride=lat_part), :] = mapped[:, at * half:(at + 1) * half]
    whole[...] = whole_w[...].reshape(lons, lat_part, half).astype(BF16)

    lon_dev = lons // groups

    def scatter(d):
        return pltpu.make_async_remote_copy(
            src_ref=whole.at[pl.ds(others[d] * lon_dev, lon_dev)],
            dst_ref=out_h.at[:, pl.ds(grp * lat_part, lat_part), :],
            send_sem=ossem.at[d], recv_sem=orsem.at[d],
            device_id={"grp": others[d]}, device_id_type=MESH,
        )

    for d in range(groups - 1):
        scatter(d).start()
    own = pltpu.make_async_copy(
        whole.at[pl.ds(grp * lon_dev, lon_dev)],
        out_h.at[:, pl.ds(grp * lat_part, lat_part), :], own_sem,
    )
    own.start()
    own.wait()
    for k in range(levels):
        ask(k).wait_send()
        pltpu.make_async_remote_copy(
            src_ref=send_v.at[k], dst_ref=recv_v.at[k],
            send_sem=ssem.at[k], recv_sem=rsem.at[k, 0],
            device_id={"lat": partners[k]}, device_id_type=MESH,
        ).wait_send()
    for d in range(groups - 1):
        pltpu.make_async_remote_copy(
            src_ref=fields.at[others[d]], dst_ref=pieces.at[grp],
            send_sem=fssem.at[d], recv_sem=frsem.at[d],
            device_id={"grp": others[d]}, device_id_type=MESH,
        ).wait_send()
        scatter(d).wait_send()
        pltpu.make_async_remote_copy(
            src_ref=whole.at[pl.ds(others[d] * lon_dev, lon_dev)],
            dst_ref=out_h.at[:, pl.ds(senders[d] * lat_part, lat_part), :],
            send_sem=ossem.at[d], recv_sem=orsem.at[d],
            device_id={"grp": others[d]}, device_id_type=MESH,
        ).wait_recv()


def on_device(coefficients, leaf, mix_self, mix_partner, skeleton, expand, slot_order):
    slots, _, columns = coefficients.shape
    width = leaf.shape[1]
    rank = mix_partner.shape[2]
    lats = expand.shape[1]
    levels = lax.axis_size("lat").bit_length() - 1
    groups = lax.axis_size("grp")
    lons = LON_DEV * groups
    half = columns // 2
    part = lats // groups
    chunks = slots // GROUP
    dma = pltpu.SemaphoreType.DMA
    anywhere = pl.BlockSpec(memory_space=pl.ANY)
    return pl.pallas_call(
        functools.partial(kernel, levels, groups, GROUP),
        out_shape=jax.ShapeDtypeStruct((LON_DEV, lats, half), BF16),
        in_specs=[anywhere] * 7,
        out_specs=anywhere,
        scratch_shapes=[
            pltpu.VMEM(coefficients.shape, BF16),
            pltpu.VMEM(leaf.shape, BF16),
            pltpu.VMEM(mix_self.shape, BF16),
            pltpu.VMEM(mix_partner.shape, BF16),
            pltpu.VMEM(expand.shape, BF16),
            pltpu.VMEM((1, groups * slots), jnp.int32),
            pltpu.VMEM((levels, slots, rank), jnp.int32),
            pltpu.VMEM((levels, slots, rank), jnp.int32),
            pltpu.VMEM((slots, width, columns), BF16),
            pltpu.VMEM((levels, slots, rank, columns), BF16),
            pltpu.VMEM((levels, slots, rank, columns), BF16),
            pltpu.VMEM((groups, slots, part, columns), BF16),
            pltpu.VMEM((groups, slots, part, columns), BF16),
            pltpu.VMEM((2, groups * slots * part, half), F32),
            pltpu.VMEM((lons * part, half), F32),
            pltpu.VMEM((lons, part, half), BF16),
            pltpu.VMEM((lons, groups * slots), BF16),
            pltpu.VMEM((lons, groups * slots), BF16),
            dma((5, chunks)), dma((2,)),
            dma((levels,)), dma((levels,)),
            dma((levels,)), dma((levels, chunks)),
            dma((groups - 1,)), dma((groups - 1,)),
            dma((groups - 1,)), dma((groups - 1,)),
            dma,
        ],
        compiler_params=pltpu.CompilerParams(
            collective_id=0, has_side_effects=True, vmem_limit_bytes=60 * 1024 * 1024
        ),
        name="synthesis",
    )(
        coefficients, leaf, mix_self, mix_partner, jnp.swapaxes(skeleton, 0, 1), expand,
        slot_order[None, :],
    )


def solution(mesh):
    return jax.shard_map(
        on_device,
        mesh=mesh,
        in_specs=(
            P("grp", "lat", None),
            P("grp", "lat", None),
            P("grp", None, "lat", None),
            P("grp", None, "lat", None),
            P("grp", None, "lat"),
            P("grp", "lat", None),
            P(),
        ),
        out_specs=P("grp", "lat", None),
        check_vma=False,
    )
```

```python
import functools
import math

import jax
import jax.numpy as jnp
from jax import lax
from jax.experimental import pallas as pl
from jax.experimental.pallas import tpu as pltpu
from jax.sharding import PartitionSpec as P

LON_DEV = 32
GROUP = 1
STRIDE = 3
AHEAD = 4
SPLIT = 3
MESH = pl.DeviceIdType.MESH
F32 = jnp.float32
BF16 = jnp.bfloat16


def dot(a, b):
    return jnp.dot(a, b, preferred_element_type=F32)


def dot_rows(a, b):
    return lax.dot_general(a, b, (((0,), (0,)), ((), ())), preferred_element_type=F32)


def kernel(
    levels, groups, gsize,
    coeff_h, leaf_h, self_h, partner_h, skel_h, expand_h, order_h, out_h,
    coeff_v, leaf_v, self_v, partner_v, expand_v,
    order_v, ask_send, ask_recv, state, send_v, recv_v,
    fields, pieces, pieces_w, whole_w, whole, cos_v, sin_v,
    in_sem, small_sem, ask_ssem, ask_rsem, ssem, rsem, fssem, frsem, ossem, orsem, own_sem,
):
    slots, width = state.shape[0], state.shape[1]
    half = coeff_v.shape[2] // 2
    chunks = slots // gsize
    lat_part = fields.shape[2]
    grp = lax.axis_index("grp")
    lat = lax.axis_index("lat")
    partners = []
    for k in range(levels):
        mask = 2**k
        partners.append(lat + (1 - 2 * ((lat // mask) % 2)) * mask)
    far = sorted(range(1, groups), key=lambda d: abs(d - groups // 2))
    others = [(grp + d) % groups for d in far]
    senders = [(grp + groups - d) % groups for d in far]

    def span(c):
        return pl.ds(c * gsize, gsize)

    loads = (
        (coeff_h, coeff_v), (leaf_h, leaf_v), (self_h, self_v),
        (partner_h, partner_v), (expand_h, expand_v),
    )

    def load(i, c):
        source, target = loads[i]
        return pltpu.make_async_copy(source.at[span(c)], target.at[span(c)], in_sem.at[i, c])

    def start_loads(c, _):
        for i in range(len(loads)):
            load(i, c).start()
        return 0

    get_skel = pltpu.make_async_copy(skel_h, ask_send, small_sem.at[0])
    get_order = pltpu.make_async_copy(order_h, order_v, small_sem.at[1])
    get_skel.start()
    get_order.start()
    for c in range(min(AHEAD, chunks)):
        start_loads(c, 0)

    barrier = pltpu.get_barrier_semaphore()
    for k in range(levels):
        pl.semaphore_signal(barrier, inc=1, device_id={"lat": partners[k]}, device_id_type=MESH)
    for other in others:
        pl.semaphore_signal(barrier, inc=1, device_id={"grp": other}, device_id_type=MESH)
    get_skel.wait()
    pl.semaphore_wait(barrier, levels + groups - 1)

    def ask(k):
        return pltpu.make_async_remote_copy(
            src_ref=ask_send.at[k], dst_ref=ask_recv.at[k],
            send_sem=ask_ssem.at[k], recv_sem=ask_rsem.at[k],
            device_id={"lat": partners[k]}, device_id_type=MESH,
        )

    for k in range(levels):
        ask(k).start()

    lons = whole.shape[0]
    total = groups * slots
    get_order.wait()
    order = order_v[...]
    turn = lax.broadcasted_iota(jnp.int32, (lons, total), 0)
    turn = (jnp.maximum(order, 0) * turn) & (lons - 1)
    angle = 2.0 * math.pi * turn.astype(F32) / lons
    scale = jnp.where(order >= 0, 1.0 / math.sqrt(total * 3 // 4), 0.0)
    cos_v[...] = (jnp.cos(angle) * scale).astype(BF16)
    sin_v[...] = (-jnp.sin(angle) * scale).astype(BF16)

    def exchange(k, c):
        return pltpu.make_async_remote_copy(
            src_ref=send_v.at[k, span(c)], dst_ref=recv_v.at[k, span(c)],
            send_sem=ssem.at[k], recv_sem=rsem.at[k, c],
            device_id={"lat": partners[k]}, device_id_type=MESH,
        )

    def hand_over(d, c):
        return pltpu.make_async_remote_copy(
            src_ref=fields.at[others[d], span(c)], dst_ref=pieces.at[grp, span(c)],
            send_sem=fssem.at[d], recv_sem=frsem.at[d],
            device_id={"grp": others[d]}, device_id_type=MESH,
        )

    row_of = lax.broadcasted_iota(jnp.int32, (width, ask_recv.shape[2]), 0)

    def stage(k, c):
        if k == 0:
            load(0, c).wait()
            load(1, c).wait()
        else:
            if k == 1:
                load(2, c).wait()
                load(3, c).wait()
            if k == levels:
                load(4, c).wait()
            exchange(k - 1, c).wait_recv()
        for i in range(gsize):
            q = c * gsize + i
            if k == 0:
                now = dot(leaf_v[q], coeff_v[q]).astype(BF16)
            else:
                mixed = dot(self_v[q, k - 1], state[q])
                mixed = mixed + dot_rows(partner_v[q, k - 1], recv_v[k - 1, q])
                now = mixed.astype(BF16)
            if k < levels and i == 0:
                @pl.when(c == 0)
                def _():
                    ask(k).wait_recv()

            if k < levels:
                wanted = ask_recv[k, pl.ds(q, 1), :]
                pick = (row_of == wanted).astype(F32).astype(BF16)
                send_v[k, q] = dot_rows(pick, now).astype(BF16)
                state[q] = now
            else:
                field = dot(expand_v[q], now).astype(BF16)
                for g in range(groups):
                    fields[g, q] = field[g * lat_part:(g + 1) * lat_part]
        if k < levels:
            exchange(k, c).start()
        else:
            for d in range(groups - 1):
                hand_over(d, c).start()

    def run(t, k):
        c = t - k * STRIDE

        @pl.when((c >= 0) & (c < chunks))
        def _():
            stage(k, c)

    core = grp % 2

    def half_step(u, _):
        t = u // 2

        @pl.when((u % 2 == 0) & (t + AHEAD < chunks))
        def _():
            start_loads(t + AHEAD, 0)

        @pl.when((u + core) % 2 == 0)
        def _():
            for k in range(SPLIT):
                run(t, k)

        @pl.when((u + core) % 2 == 1)
        def _():
            for k in range(SPLIT, levels + 1):
                run(t, k)

        return 0

    lax.fori_loop(0, 2 * (chunks + levels * STRIDE), half_step, 0)

    def widen(block, value):
        rows = slots * lat_part
        flat = value.astype(F32).reshape(rows, 2 * half)
        for part in range(2):
            pieces_w[part, pl.ds(block * rows, rows), :] = flat[:, part * half:(part + 1) * half]

    widen(grp, fields[grp])
    for d in range(groups - 1):
        pltpu.make_async_remote_copy(
            src_ref=fields.at[others[d]], dst_ref=pieces.at[senders[d]],
            send_sem=fssem.at[d], recv_sem=frsem.at[d],
            device_id={"grp": others[d]}, device_id_type=MESH,
        ).wait_recv()
        widen(senders[d], pieces[senders[d]])

    cos_table, sin_table = cos_v[...], sin_v[...]
    for row in range(0, lat_part, 2):
        parts = []
        for part in range(2):
            pair = [pieces_w[part, pl.ds(row + at, total, stride=lat_part), :] for at in range(2)]
            parts.append(jnp.concatenate(pair, axis=1).astype(BF16))
        mapped = dot(cos_table, parts[0]) + dot(sin_table, parts[1])
        for at in range(2):
            whole_w[pl.ds(row + at, lons, stride=lat_part), :] = mapped[:, at * half:(at + 1) * half]
    whole[...] = whole_w[...].reshape(lons, lat_part, half).astype(BF16)

    lon_dev = lons // groups

    def scatter(d):
        return pltpu.make_async_remote_copy(
            src_ref=whole.at[pl.ds(others[d] * lon_dev, lon_dev)],
            dst_ref=out_h.at[:, pl.ds(grp * lat_part, lat_part), :],
            send_sem=ossem.at[d], recv_sem=orsem.at[d],
            device_id={"grp": others[d]}, device_id_type=MESH,
        )

    for d in range(groups - 1):
        scatter(d).start()
    own = pltpu.make_async_copy(
        whole.at[pl.ds(grp * lon_dev, lon_dev)],
        out_h.at[:, pl.ds(grp * lat_part, lat_part), :], own_sem,
    )
    own.start()
    own.wait()
    for k in range(levels):
        ask(k).wait_send()
        pltpu.make_async_remote_copy(
            src_ref=send_v.at[k], dst_ref=recv_v.at[k],
            send_sem=ssem.at[k], recv_sem=rsem.at[k, 0],
            device_id={"lat": partners[k]}, device_id_type=MESH,
        ).wait_send()
    for d in range(groups - 1):
        pltpu.make_async_remote_copy(
            src_ref=fields.at[others[d]], dst_ref=pieces.at[grp],
            send_sem=fssem.at[d], recv_sem=frsem.at[d],
            device_id={"grp": others[d]}, device_id_type=MESH,
        ).wait_send()
        scatter(d).wait_send()
        pltpu.make_async_remote_copy(
            src_ref=whole.at[pl.ds(others[d] * lon_dev, lon_dev)],
            dst_ref=out_h.at[:, pl.ds(senders[d] * lat_part, lat_part), :],
            send_sem=ossem.at[d], recv_sem=orsem.at[d],
            device_id={"grp": others[d]}, device_id_type=MESH,
        ).wait_recv()


def on_device(coefficients, leaf, mix_self, mix_partner, skeleton, expand, slot_order):
    slots, _, columns = coefficients.shape
    width = leaf.shape[1]
    rank = mix_partner.shape[2]
    lats = expand.shape[1]
    levels = lax.axis_size("lat").bit_length() - 1
    groups = lax.axis_size("grp")
    lons = LON_DEV * groups
    half = columns // 2
    part = lats // groups
    chunks = slots // GROUP
    dma = pltpu.SemaphoreType.DMA
    anywhere = pl.BlockSpec(memory_space=pl.ANY)
    return pl.pallas_call(
        functools.partial(kernel, levels, groups, GROUP),
        out_shape=jax.ShapeDtypeStruct((LON_DEV, lats, half), BF16),
        in_specs=[pl.BlockSpec(memory_space=pltpu.HBM)] * 7,
        out_specs=anywhere,
        scratch_shapes=[
            pltpu.VMEM(coefficients.shape, BF16),
            pltpu.VMEM(leaf.shape, BF16),
            pltpu.VMEM(mix_self.shape, BF16),
            pltpu.VMEM(mix_partner.shape, BF16),
            pltpu.VMEM(expand.shape, BF16),
            pltpu.VMEM((1, groups * slots), jnp.int32),
            pltpu.VMEM((levels, slots, rank), jnp.int32),
            pltpu.VMEM((levels, slots, rank), jnp.int32),
            pltpu.VMEM((slots, width, columns), BF16),
            pltpu.VMEM((levels, slots, rank, columns), BF16),
            pltpu.VMEM((levels, slots, rank, columns), BF16),
            pltpu.VMEM((groups, slots, part, columns), BF16),
            pltpu.VMEM((groups, slots, part, columns), BF16),
            pltpu.VMEM((2, groups * slots * part, half), F32),
            pltpu.VMEM((lons * part, half), F32),
            pltpu.VMEM((lons, part, half), BF16),
            pltpu.VMEM((lons, groups * slots), BF16),
            pltpu.VMEM((lons, groups * slots), BF16),
            dma((5, chunks)), dma((2,)),
            dma((levels,)), dma((levels,)),
            dma((levels,)), dma((levels, chunks)),
            dma((groups - 1,)), dma((groups - 1,)),
            dma((groups - 1,)), dma((groups - 1,)),
            dma,
        ],
        compiler_params=pltpu.CompilerParams(
            collective_id=0, has_side_effects=True, vmem_limit_bytes=60 * 1024 * 1024
        ),
        name="synthesis",
    )(
        coefficients, leaf, mix_self, mix_partner, jnp.swapaxes(skeleton, 0, 1), expand,
        slot_order[None, :],
    )


def solution(mesh):
    return jax.shard_map(
        on_device,
        mesh=mesh,
        in_specs=(
            P("grp", "lat", None),
            P("grp", "lat", None),
            P("grp", None, "lat", None),
            P("grp", None, "lat", None),
            P("grp", None, "lat"),
            P("grp", "lat", None),
            P(),
        ),
        out_specs=P("grp", "lat", None),
        check_vma=False,
    )
```

```python
import functools
import math

import jax
import jax.numpy as jnp
from jax import lax
from jax.experimental import pallas as pl
from jax.experimental.pallas import tpu as pltpu
from jax.sharding import PartitionSpec as P

LON_DEV = 32
GROUP = 1
STRIDE = 3
AHEAD = 4
SPLIT = 3
MESH = pl.DeviceIdType.MESH
F32 = jnp.float32
BF16 = jnp.bfloat16


def dot(a, b):
    return jnp.dot(a, b, preferred_element_type=F32)


def dot_rows(a, b):
    return lax.dot_general(a, b, (((0,), (0,)), ((), ())), preferred_element_type=F32)


def kernel(
    levels, groups, gsize,
    coeff_h, leaf_h, self_h, partner_h, skel_h, expand_h, order_h, out_h,
    coeff_v, leaf_v, self_v, partner_v, expand_v,
    order_v, ask_send, ask_recv, state, send_v, recv_v,
    fields, pieces, pieces_w, whole_w, whole, cos_v, sin_v,
    in_sem, small_sem, ask_ssem, ask_rsem, ssem, rsem, fssem, frsem, ossem, orsem, own_sem,
):
    slots, width = state.shape[0], state.shape[1]
    half = coeff_v.shape[2] // 2
    chunks = slots // gsize
    lat_part = fields.shape[2]
    grp = lax.axis_index("grp")
    lat = lax.axis_index("lat")
    partners = []
    for k in range(levels):
        mask = 2**k
        partners.append(lat + (1 - 2 * ((lat // mask) % 2)) * mask)
    far = sorted(range(1, groups), key=lambda d: abs(d - groups // 2))
    others = [(grp + d) % groups for d in far]
    senders = [(grp + groups - d) % groups for d in far]

    barrier = pltpu.get_barrier_semaphore()
    for k in range(levels):
        pl.semaphore_signal(barrier, inc=1, device_id={"lat": partners[k]}, device_id_type=MESH)
    for other in others:
        pl.semaphore_signal(barrier, inc=1, device_id={"grp": other}, device_id_type=MESH)

    def span(c):
        return pl.ds(c * gsize, gsize)

    loads = (
        (coeff_h, coeff_v), (leaf_h, leaf_v), (self_h, self_v),
        (partner_h, partner_v), (expand_h, expand_v),
    )

    def load(i, c):
        source, target = loads[i]
        return pltpu.make_async_copy(source.at[span(c)], target.at[span(c)], in_sem.at[i, c])

    def start_loads(c, _):
        for i in range(len(loads)):
            load(i, c).start()
        return 0

    get_skel = pltpu.make_async_copy(skel_h, ask_send, small_sem.at[0])
    get_order = pltpu.make_async_copy(order_h, order_v, small_sem.at[1])
    get_skel.start()
    get_order.start()
    for c in range(min(AHEAD, chunks)):
        start_loads(c, 0)

    get_skel.wait()
    pl.semaphore_wait(barrier, levels + groups - 1)

    def ask(k):
        return pltpu.make_async_remote_copy(
            src_ref=ask_send.at[k], dst_ref=ask_recv.at[k],
            send_sem=ask_ssem.at[k], recv_sem=ask_rsem.at[k],
            device_id={"lat": partners[k]}, device_id_type=MESH,
        )

    for k in range(levels):
        ask(k).start()

    lons = whole.shape[0]
    total = groups * slots
    get_order.wait()
    order = order_v[...]
    turn = lax.broadcasted_iota(jnp.int32, (lons, total), 0)
    turn = (jnp.maximum(order, 0) * turn) & (lons - 1)
    angle = 2.0 * math.pi * turn.astype(F32) / lons
    scale = jnp.where(order >= 0, 1.0 / math.sqrt(total * 3 // 4), 0.0)
    cos_v[...] = (jnp.cos(angle) * scale).astype(BF16)
    sin_v[...] = (-jnp.sin(angle) * scale).astype(BF16)

    def exchange(k, c):
        return pltpu.make_async_remote_copy(
            src_ref=send_v.at[k, span(c)], dst_ref=recv_v.at[k, span(c)],
            send_sem=ssem.at[k], recv_sem=rsem.at[k, c],
            device_id={"lat": partners[k]}, device_id_type=MESH,
        )

    def hand_over(d, c):
        return pltpu.make_async_remote_copy(
            src_ref=fields.at[others[d], span(c)], dst_ref=pieces.at[grp, span(c)],
            send_sem=fssem.at[d], recv_sem=frsem.at[d],
            device_id={"grp": others[d]}, device_id_type=MESH,
        )

    row_of = lax.broadcasted_iota(jnp.int32, (width, ask_recv.shape[2]), 0)

    def stage(k, c):
        if k == 0:
            load(0, c).wait()
            load(1, c).wait()
        else:
            if k == 1:
                load(2, c).wait()
                load(3, c).wait()
            if k == levels:
                load(4, c).wait()
            exchange(k - 1, c).wait_recv()
        for i in range(gsize):
            q = c * gsize + i
            if k == 0:
                now = dot(leaf_v[q], coeff_v[q]).astype(BF16)
            else:
                mixed = dot(self_v[q, k - 1], state[q])
                mixed = mixed + dot_rows(partner_v[q, k - 1], recv_v[k - 1, q])
                now = mixed.astype(BF16)
            if k < levels and i == 0:
                @pl.when(c == 0)
                def _():
                    ask(k).wait_recv()

            if k < levels:
                wanted = ask_recv[k, pl.ds(q, 1), :]
                pick = (row_of == wanted).astype(F32).astype(BF16)
                send_v[k, q] = dot_rows(pick, now).astype(BF16)
                state[q] = now
            else:
                field = dot(expand_v[q], now).astype(BF16)
                for g in range(groups):
                    fields[g, q] = field[g * lat_part:(g + 1) * lat_part]
        if k < levels:
            exchange(k, c).start()
        else:
            for d in range(groups - 1):
                hand_over(d, c).start()

    def run(t, k):
        c = t - k * STRIDE

        @pl.when((c >= 0) & (c < chunks))
        def _():
            stage(k, c)

    core = grp % 2

    def half_step(u, _):
        t = u // 2

        @pl.when((u % 2 == 0) & (t + AHEAD < chunks))
        def _():
            start_loads(t + AHEAD, 0)

        @pl.when((u + core) % 2 == 0)
        def _():
            for k in range(SPLIT):
                run(t, k)

        @pl.when((u + core) % 2 == 1)
        def _():
            for k in range(SPLIT, levels + 1):
                run(t, k)

        return 0

    lax.fori_loop(0, 2 * (chunks + levels * STRIDE), half_step, 0)

    def widen(block, value):
        rows = slots * lat_part
        flat = value.astype(F32).reshape(rows, 2 * half)
        for part in range(2):
            pieces_w[part, pl.ds(block * rows, rows), :] = flat[:, part * half:(part + 1) * half]

    widen(grp, fields[grp])
    for d in range(groups - 1):
        pltpu.make_async_remote_copy(
            src_ref=fields.at[others[d]], dst_ref=pieces.at[senders[d]],
            send_sem=fssem.at[d], recv_sem=frsem.at[d],
            device_id={"grp": others[d]}, device_id_type=MESH,
        ).wait_recv()
        widen(senders[d], pieces[senders[d]])

    cos_table, sin_table = cos_v[...], sin_v[...]
    for row in range(0, lat_part, 2):
        parts = []
        for part in range(2):
            pair = [pieces_w[part, pl.ds(row + at, total, stride=lat_part), :] for at in range(2)]
            parts.append(jnp.concatenate(pair, axis=1).astype(BF16))
        mapped = dot(cos_table, parts[0]) + dot(sin_table, parts[1])
        for at in range(2):
            whole_w[pl.ds(row + at, lons, stride=lat_part), :] = mapped[:, at * half:(at + 1) * half]
    whole[...] = whole_w[...].reshape(lons, lat_part, half).astype(BF16)

    lon_dev = lons // groups

    def scatter(d):
        return pltpu.make_async_remote_copy(
            src_ref=whole.at[pl.ds(others[d] * lon_dev, lon_dev)],
            dst_ref=out_h.at[:, pl.ds(grp * lat_part, lat_part), :],
            send_sem=ossem.at[d], recv_sem=orsem.at[d],
            device_id={"grp": others[d]}, device_id_type=MESH,
        )

    for d in range(groups - 1):
        scatter(d).start()
    own = pltpu.make_async_copy(
        whole.at[pl.ds(grp * lon_dev, lon_dev)],
        out_h.at[:, pl.ds(grp * lat_part, lat_part), :], own_sem,
    )
    own.start()
    own.wait()
    for k in range(levels):
        ask(k).wait_send()
        pltpu.make_async_remote_copy(
            src_ref=send_v.at[k], dst_ref=recv_v.at[k],
            send_sem=ssem.at[k], recv_sem=rsem.at[k, 0],
            device_id={"lat": partners[k]}, device_id_type=MESH,
        ).wait_send()
    for d in range(groups - 1):
        pltpu.make_async_remote_copy(
            src_ref=fields.at[others[d]], dst_ref=pieces.at[grp],
            send_sem=fssem.at[d], recv_sem=frsem.at[d],
            device_id={"grp": others[d]}, device_id_type=MESH,
        ).wait_send()
        scatter(d).wait_send()
        pltpu.make_async_remote_copy(
            src_ref=whole.at[pl.ds(others[d] * lon_dev, lon_dev)],
            dst_ref=out_h.at[:, pl.ds(senders[d] * lat_part, lat_part), :],
            send_sem=ossem.at[d], recv_sem=orsem.at[d],
            device_id={"grp": others[d]}, device_id_type=MESH,
        ).wait_recv()


def on_device(coefficients, leaf, mix_self, mix_partner, skeleton, expand, slot_order):
    slots, _, columns = coefficients.shape
    width = leaf.shape[1]
    rank = mix_partner.shape[2]
    lats = expand.shape[1]
    levels = lax.axis_size("lat").bit_length() - 1
    groups = lax.axis_size("grp")
    lons = LON_DEV * groups
    half = columns // 2
    part = lats // groups
    chunks = slots // GROUP
    dma = pltpu.SemaphoreType.DMA
    anywhere = pl.BlockSpec(memory_space=pl.ANY)
    return pl.pallas_call(
        functools.partial(kernel, levels, groups, GROUP),
        out_shape=jax.ShapeDtypeStruct((LON_DEV, lats, half), BF16),
        in_specs=[pl.BlockSpec(memory_space=pltpu.HBM)] * 7,
        out_specs=anywhere,
        scratch_shapes=[
            pltpu.VMEM(coefficients.shape, BF16),
            pltpu.VMEM(leaf.shape, BF16),
            pltpu.VMEM(mix_self.shape, BF16),
            pltpu.VMEM(mix_partner.shape, BF16),
            pltpu.VMEM(expand.shape, BF16),
            pltpu.VMEM((1, groups * slots), jnp.int32),
            pltpu.VMEM((levels, slots, rank), jnp.int32),
            pltpu.VMEM((levels, slots, rank), jnp.int32),
            pltpu.VMEM((slots, width, columns), BF16),
            pltpu.VMEM((levels, slots, rank, columns), BF16),
            pltpu.VMEM((levels, slots, rank, columns), BF16),
            pltpu.VMEM((groups, slots, part, columns), BF16),
            pltpu.VMEM((groups, slots, part, columns), BF16),
            pltpu.VMEM((2, groups * slots * part, half), F32),
            pltpu.VMEM((lons * part, half), F32),
            pltpu.VMEM((lons, part, half), BF16),
            pltpu.VMEM((lons, groups * slots), BF16),
            pltpu.VMEM((lons, groups * slots), BF16),
            dma((5, chunks)), dma((2,)),
            dma((levels,)), dma((levels,)),
            dma((levels,)), dma((levels, chunks)),
            dma((groups - 1,)), dma((groups - 1,)),
            dma((groups - 1,)), dma((groups - 1,)),
            dma,
        ],
        compiler_params=pltpu.CompilerParams(
            collective_id=0, has_side_effects=True, vmem_limit_bytes=60 * 1024 * 1024
        ),
        name="synthesis",
    )(
        coefficients, leaf, mix_self, mix_partner, jnp.swapaxes(skeleton, 0, 1), expand,
        slot_order[None, :],
    )


def solution(mesh):
    return jax.shard_map(
        on_device,
        mesh=mesh,
        in_specs=(
            P("grp", "lat", None),
            P("grp", "lat", None),
            P("grp", None, "lat", None),
            P("grp", None, "lat", None),
            P("grp", None, "lat"),
            P("grp", "lat", None),
            P(),
        ),
        out_specs=P("grp", "lat", None),
        check_vma=False,
    )
```
